32 devices in a mesh: dp: 16 (over z, x, core), fsdp: 2 (over y).
Axes of the slice: x: 2, y: 2, z: 4, core: 2. Of those that a mesh axis runs over, the one named last changes fastest.
Arguments:
- tokens: bfloat16 [32, 1024, 1024], P(('dp', 'fsdp')), may hold values from -6 to 6
- w_qkv: bfloat16 [1024, 3072], P(('dp', 'fsdp')), may hold values from -0.1875 to 0.1875
- w_out: bfloat16 [1024, 1024], P(('dp', 'fsdp')), may hold values from -0.1875 to 0.1875
- w_up: bfloat16 [1024, 4096], P(('dp', 'fsdp')), may hold values from -0.1875 to 0.1875
- w_down: bfloat16 [4096, 1024], P(('dp', 'fsdp')), may hold values from -0.09375 to 0.09375
- gain_one: bfloat16 [1024], P('fsdp'), may hold values from 0.5 to 1.5
- shift_one: bfloat16 [1024], P('fsdp'), may hold values from -1.1953125 to 1.1953125
- gain_two: bfloat16 [1024], P('fsdp'), may hold values from 0.5 to 1.5
- attention_norm_bias: bfloat16 [1024], P('fsdp'), may hold values from -1.1953125 to 1.1953125
- gain_three: bfloat16 [1024], P('fsdp'), may hold values from 0.5 to 1.5
- shift_three: bfloat16 [1024], P('fsdp'), may hold values from -1.1953125 to 1.1953125
- gain_four: bfloat16 [1024], P('fsdp'), may hold values from 0.5 to 1.5
- shift_four: bfloat16 [1024], P('fsdp'), may hold values from -1.1953125 to 1.1953125
- group_ids: int32 [32], P(('dp', 'fsdp')), may hold values from 0 to 7
- group_weight: float32 [8], replicated, may hold values from 0.3 to 3
- out_grad: bfloat16 [32, 1024, 1024], P(('dp', 'fsdp')), may hold values from -6 to 6
Outputs:
- activations: bfloat16 [32, 1024, 1024], P(('dp', 'fsdp'))
- input_grad: float32 [32, 1024, 1024], P(('dp', 'fsdp'))
- grad_qkv: float32 [1024, 3072], P(('dp', 'fsdp'))
- grad_out: float32 [1024, 1024], P(('dp', 'fsdp'))
- grad_up: float32 [1024, 4096], P(('dp', 'fsdp'))
- grad_down: float32 [4096, 1024], P(('dp', 'fsdp'))
- grad_gain_one: float32 [1024], P('fsdp')
- grad_shift_one: float32 [1024], P('fsdp')
- grad_gain_two: float32 [1024], P('fsdp')
- grad_shift_two: float32 [1024], P('fsdp')
- grad_gain_three: float32 [1024], P('fsdp')
- grad_shift_three: float32 [1024], P('fsdp')
- grad_gain_four: float32 [1024], P('fsdp')
- grad_shift_four: float32 [1024], P('fsdp')
The draws below stay inside these ranges and needn't reach their ends.
All inputs are finite; a program needn't handle non-finite values.
Results may differ from the reference program's by a relative error of at most 0.015.
Values may be sent and summed in bfloat16 or wider, within the bound.
No kernel may reach another device: no remote copies, remote signals or barrier semaphores. Data moves between devices by JAX's collectives and lax.ppermute only.
A program may use at most 256 MiB of HBM per device.

```python
import math
import jax
import jax.numpy as jnp
from jax import lax

D = 1024
FF = 4096
HEAD = 64
LEN = 1024
GROUPS = 8
BATCH = 32


def with_ends(drawn, key, smallest, top_value):
    index_at = [jax.random.randint(jax.random.fold_in(key, axis), (), 0, length) for axis, length in enumerate(drawn.shape)]
    longest = drawn.shape.index(max(drawn.shape))
    beside = index_at[:longest] + [(index_at[longest] + 1) % drawn.shape[longest]] + index_at[longest + 1:]
    return drawn.at[tuple(index_at)].set(smallest).at[tuple(beside)].set(top_value)


def block_levels(own_key, extent, pieces, smallest, largest):
    def one(dim, shards_of):
        heights = jax.random.uniform(jax.random.fold_in(jax.random.fold_in(own_key, 6), dim), (shards_of,), jnp.float32, smallest / len(pieces), largest / len(pieces))
        return jnp.repeat(jnp.exp(heights), extent[dim] // shards_of).reshape((-1,) + (1,) * (len(extent) - dim - 1))

    level = one(*pieces[0])
    for cut in pieces[1:]:
        level = level * one(*cut)
    return level


def normal_values(key, extent, scale, bound, shards=(), held_as=jnp.bfloat16):
    array = scale * jax.random.normal(key, extent, jnp.float32)
    if shards:
        array = array * block_levels(key, extent, shards, -0.22, 0.18)
    return jnp.clip(array, -bound, bound).astype(held_as)


def setup_inputs(seed: int = 0) -> dict:
    key_of = jax.random.split(jax.random.key(seed), 17)
    tokens = normal_values(key_of[0], (BATCH, LEN, D), 1.0, 6.0, ((0, 32),))
    w_qkv = normal_values(key_of[1], (D, 3 * D), D ** -0.5, 0.1875, ((0, 32),))
    w_out = normal_values(key_of[2], (D, D), D ** -0.5, 0.1875, ((0, 32),))
    w_up = normal_values(key_of[3], (D, FF), D ** -0.5, 0.1875, ((0, 32),))
    w_down = normal_values(key_of[4], (FF, D), FF ** -0.5, 0.09375, ((0, 32),))
    gain_one = jnp.clip(1.0 + 0.1 * jax.random.normal(key_of[5], (D,), jnp.float32), 0.5, 1.5).astype(jnp.bfloat16)
    shift_one = normal_values(key_of[6], (D,), 0.3, 1.1953125, ((0, 2),))
    gain_two = jnp.clip(1.0 + 0.1 * jax.random.normal(key_of[7], (D,), jnp.float32), 0.5, 1.5).astype(jnp.bfloat16)
    attention_norm_bias = normal_values(key_of[8], (D,), 0.3, 1.1953125, ((0, 2),))
    gain_three = jnp.clip(1.0 + 0.1 * jax.random.normal(key_of[9], (D,), jnp.float32), 0.5, 1.5).astype(jnp.bfloat16)
    shift_three = normal_values(key_of[10], (D,), 0.3, 1.1953125, ((0, 2),))
    gain_four = jnp.clip(1.0 + 0.1 * jax.random.normal(key_of[11], (D,), jnp.float32), 0.5, 1.5).astype(jnp.bfloat16)
    shift_four = normal_values(key_of[12], (D,), 0.3, 1.1953125, ((0, 2),))
    group_ids = with_ends(jax.random.randint(key_of[13], (BATCH,), 0, GROUPS), jax.random.fold_in(key_of[13], 1), 0, GROUPS - 1).astype(jnp.int32)
    group_weight = jnp.clip(jnp.exp(jax.random.uniform(key_of[14], (GROUPS,), jnp.float32, math.log(0.3), math.log(3.0))), 0.3, 3.0)
    out_grad = normal_values(key_of[15], (BATCH, LEN, D), 1.0, 6.0, ((0, 32),))
    return dict(tokens=tokens, w_qkv=w_qkv, w_out=w_out, w_up=w_up, w_down=w_down, gain_one=gain_one, shift_one=shift_one, gain_two=gain_two, attention_norm_bias=attention_norm_bias, gain_three=gain_three, shift_three=shift_three, gain_four=gain_four, shift_four=shift_four, group_ids=group_ids, group_weight=group_weight, out_grad=out_grad)


@jax.custom_vjp
def low(v):
    return lax.optimization_barrier(v.astype(jnp.bfloat16)).astype(jnp.float32)

@jax.custom_vjp
def low_back(v):
    return v

def low_keep(v):
    return (low(v), None)

def low_pass(kept, grad):
    return (grad,)

def back_keep(v):
    return (v, None)

def back_low(kept, grad):
    return (low(grad),)
low.defvjp(low_keep, low_pass)
low_back.defvjp(back_keep, back_low)
epsilon = 1e-05
highest_precision = lax.Precision.HIGHEST

def layer_norm(value_vectors, gain, shift):
    center = lax.optimization_barrier(jnp.mean(value_vectors, axis=-1, keepdims=True))
    position_offset = value_vectors - center
    spread = lax.optimization_barrier(jnp.mean(position_offset * position_offset, axis=-1, keepdims=True))
    return position_offset * lax.rsqrt(spread + epsilon) * gain + shift

def rotary_tables(length, half):
    places = jnp.arange(length, dtype=jnp.float32)[:, None]
    speeds = jnp.exp(jnp.arange(half, dtype=jnp.float32) * (-math.log(10000.0) / half))
    angles = places * speeds[None, :]
    return (jnp.cos(angles), jnp.sin(angles))

def rotate(value_vectors, cosine, sine):
    half = value_vectors.shape[-1] // 2
    first_half = value_vectors[..., :half]
    second_half = value_vectors[..., half:]
    cosine = cosine[:, None, :]
    sine = sine[:, None, :]
    return jnp.concatenate([first_half * cosine - second_half * sine, second_half * cosine + first_half * sine], axis=-1)

def project(value_vectors, weight_factor):
    return jnp.einsum('jum,my->juy', value_vectors, weight_factor, precision=highest_precision)

def forward(group_tokens, w_qkv, w_out, w_up, w_down, gain_one, shift_one, gain_two, attention_norm_bias, gain_three, shift_three, gain_four, shift_four):
    seqs, length, width = group_tokens.shape
    heads = width // HEAD
    normed_one = low(layer_norm(group_tokens, gain_one, shift_one))
    mixed = low_back(project(normed_one, w_qkv))
    cosine, sine = rotary_tables(length, HEAD // 2)
    queries = low(rotate(mixed[..., :width].reshape(seqs, length, heads, HEAD), cosine, sine))
    key_rows = low(rotate(mixed[..., width:2 * width].reshape(seqs, length, heads, HEAD), cosine, sine))
    value_rows = low(mixed[..., 2 * width:].reshape(seqs, length, heads, HEAD))
    block = min(512, length)
    factor = HEAD ** (-0.5)

    def attend(start):
        query_block = lax.dynamic_slice_in_dim(queries, start, block, 1)
        scores = jnp.einsum('sqhe,skhe->shqk', query_block, key_rows, precision=highest_precision) * factor
        scores = low_back(scores)
        rows_at = start + jnp.arange(block, dtype=jnp.int32)[:, None]
        cols_at = jnp.arange(length, dtype=jnp.int32)[None, :]
        scores = jnp.where(cols_at <= rows_at, scores, -1e+30)
        row_maximum_score = lax.optimization_barrier(jnp.max(scores, axis=-1, keepdims=True))
        raised_exponent = jnp.exp(scores - row_maximum_score)
        probs = low(raised_exponent / lax.optimization_barrier(jnp.sum(raised_exponent, axis=-1, keepdims=True)))
        return jnp.einsum('shqk,skhe->sqhe', probs, value_rows, precision=highest_precision)
    starts = (jnp.arange(length // block, dtype=jnp.int32) * block).astype(jnp.int32)
    blocks = lax.map(jax.checkpoint(attend), starts)
    attended = jnp.moveaxis(blocks, 0, 1).reshape(seqs, length, width)
    attended = low_back(low(attended))
    branch_one = low_back(project(attended, w_out))
    after_one = group_tokens + layer_norm(branch_one, gain_two, attention_norm_bias)
    normed_two = low(layer_norm(after_one, gain_three, shift_three))
    hidden = low_back(project(normed_two, w_up))
    active = low(jax.nn.gelu(hidden, approximate=True))
    branch_two = low_back(project(active, w_down))
    return after_one + layer_norm(branch_two, gain_four, shift_four)

def reference(tokens, w_qkv, w_out, w_up, w_down, gain_one, shift_one, gain_two, attention_norm_bias, gain_three, shift_three, gain_four, shift_four, group_ids, group_weight, out_grad):
    params = tuple((member.astype(jnp.float32) for member in (w_qkv, w_out, w_up, w_down, gain_one, shift_one, gain_two, attention_norm_bias, gain_three, shift_three, gain_four, shift_four)))
    group_size = math.gcd(BATCH, max(1, 4096 // LEN))
    group_count = BATCH // group_size
    scales = jnp.take(group_weight.astype(jnp.float32), group_ids.astype(jnp.int32))
    cotangent = out_grad.astype(jnp.float32) * scales[:, None, None]
    inputs = tokens.astype(jnp.float32).reshape(group_count, group_size, LEN, D)
    cotangent = cotangent.reshape(group_count, group_size, LEN, D)

    def accumulate(totals, member):
        group_tokens, group_cot = member
        result, pullback = jax.vjp(forward, group_tokens, *params)
        gradients = pullback(group_cot)
        totals = tuple((running + fresh for running, fresh in zip(totals, gradients[1:])))
        return (totals, (result.astype(jnp.bfloat16), gradients[0]))
    zeros = tuple((jnp.zeros(member.shape, jnp.float32) for member in params))
    totals, (results, input_grads) = lax.scan(accumulate, zeros, (inputs, cotangent))
    return (results.reshape(BATCH, LEN, D), input_grads.reshape(BATCH, LEN, D), totals[0], totals[1], totals[2], totals[3], totals[4], totals[5], totals[6], totals[7], totals[8], totals[9], totals[10], totals[11])
```

```python
import math

import jax
import jax.numpy as jnp
from jax import lax
from jax.experimental import pallas as pl
from jax.experimental.pallas import tpu as pltpu
from jax.sharding import PartitionSpec as P

HEAD = 64
GROUPS = 8
QB = 256

epsilon = 1e-05
bf16 = jnp.bfloat16
f32 = jnp.float32
NT = (((1,), (1,)), ((), ()))
NN = (((1,), (0,)), ((), ()))
TN = (((0,), (0,)), ((), ()))


def dot(a, b, dims):
    return lax.dot_general(a, b, dims, preferred_element_type=f32)


class Bit:
    def __init__(self, axis, size, place, weight):
        self.axis, self.place, self.weight = axis, place, weight
        self.pairs = [(i, i ^ (1 << place)) for i in range(size)]

    def mine(self):
        return (lax.axis_index(self.axis) >> self.place) & 1

    def swap(self, value):
        return lax.ppermute(value, self.axis, self.pairs)


def all_bits(dp, fsdp):
    low = fsdp.bit_length() - 1
    outer = [Bit("dp", dp, k, low + k) for k in range(dp.bit_length() - 1)]
    inner = [Bit("fsdp", fsdp, k, k) for k in range(low)]
    return outer, inner


def gather_rows(shard, bits):
    held = []
    value = shard
    for bit in bits:
        other = bit.swap(value)
        mine = bit.mine() == 0
        spot = sum(1 for w in held if w > bit.weight)
        value = jnp.stack([jnp.where(mine, value, other), jnp.where(mine, other, value)], axis=spot)
        held = sorted(held + [bit.weight], reverse=True)
    return value.reshape((-1,) + shard.shape[1:])


def reduce_rows(total, bits):
    left = sorted([b.weight for b in bits], reverse=True)
    rows = total.shape[0] >> len(bits)
    value = total.reshape((2,) * len(bits) + (rows,) + total.shape[1:])
    for at, bit in enumerate(bits):
        spot = left.index(bit.weight)
        mine = bit.mine()
        send = lax.dynamic_index_in_dim(value, 1 - mine, spot, keepdims=False)
        keep = lax.dynamic_index_in_dim(value, mine, spot, keepdims=False)
        value = keep.astype(f32) + bit.swap(send).astype(f32)
        if at + 1 < len(bits):
            value = value.astype(bf16)
        left.remove(bit.weight)
    return value


def spread_vectors(packed, inner):
    value = packed[None]
    for bit in inner:
        other = bit.swap(value)
        mine = bit.mine() == 0
        value = jnp.concatenate([jnp.where(mine, value, other), jnp.where(mine, other, value)], axis=0)
    return jnp.moveaxis(value, 0, 1).reshape(packed.shape[0], -1)


def sum_vectors(packed, outer, inner):
    count, width = packed.shape
    value = jnp.moveaxis(packed.reshape(count, 1 << len(inner), -1), 1, 0)
    for bit in reversed(inner):
        half = value.shape[0] // 2
        mine = bit.mine()
        send = lax.dynamic_slice_in_dim(value, (1 - mine) * half, half, 0)
        keep = lax.dynamic_slice_in_dim(value, mine * half, half, 0)
        value = keep + bit.swap(send)
    value = value[0]
    for bit in outer:
        value = value + bit.swap(value)
    return value


def qkv_kernel(x_ref, g_ref, s_ref, w_ref, cos_ref, sin_ref, n_ref, y_ref):
    step = pl.program_id(0)
    third = pl.num_programs(0) // 3
    rows = x_ref.shape[0]
    lane = lax.broadcasted_iota(jnp.int32, (1, 128), 1)
    low32 = (lane % HEAD) < HEAD // 2

    @pl.when(step == 0)
    def _():
        for r0 in range(0, rows, QB):
            x = x_ref[r0:r0 + QB, :].astype(f32)
            c = x - jnp.mean(x, axis=-1, keepdims=True)
            r = lax.rsqrt(jnp.mean(c * c, axis=-1, keepdims=True) + epsilon)
            n_ref[r0:r0 + QB, :] = (c * r * g_ref[...] + s_ref[...]).astype(bf16)

    def product(r0):
        return dot(n_ref[r0:r0 + QB, :], w_ref[...], NN)

    @pl.when(step < 2 * third)
    def _():
        scale = jnp.where(step < third, HEAD ** -0.5, 1.0).astype(f32)
        for r0 in range(0, rows, QB):
            y = product(r0)
            cos = cos_ref[r0:r0 + QB, :] * scale
            sin = sin_ref[r0:r0 + QB, :] * scale
            for c0 in range(0, y.shape[1], 128):
                part = y[:, c0:c0 + 128]
                y_ref[r0:r0 + QB, c0:c0 + 128] = turn(part, cos, sin, low32).astype(bf16)

    @pl.when(step >= 2 * third)
    def _():
        for r0 in range(0, rows, QB):
            y_ref[r0:r0 + QB, :] = product(r0).astype(bf16)


def turn(x, cos, sin, low32):
    other = jnp.where(low32, pltpu.roll(x, 96, 1), pltpu.roll(x, 32, 1))
    return x * cos + other * sin


def qkv_call(x, gain, shift, w, cos, sin):
    rows, width = x.shape
    cols = w.shape[1]
    n = 512
    const = lambda shape: pl.BlockSpec(shape, lambda j: (0, 0))
    return pl.pallas_call(
        qkv_kernel,
        grid=(cols // n,),
        in_specs=[const((rows, width)), const((1, width)), const((1, width)),
                  pl.BlockSpec((width, n), lambda j: (0, j)), const((rows, 128)), const((rows, 128))],
        out_specs=[const((rows, width)), pl.BlockSpec((rows, n), lambda j: (0, j))],
        out_shape=[jax.ShapeDtypeStruct((rows, width), bf16), jax.ShapeDtypeStruct((rows, cols), bf16)],
        cost_estimate=pl.CostEstimate(flops=2 * rows * width * cols, transcendentals=rows,
                                      bytes_accessed=2 * (2 * rows * width + width * cols + rows * cols)),
        name="qkv_forward",
    )(x, gain, shift, w, cos, sin)

def attn_fwd_kernel(q_ref, k_ref, v_ref, o_ref, lse_ref):
    length = q_ref.shape[0]
    lane = lax.broadcasted_iota(jnp.int32, (1, 128), 1)
    low = lane < 64
    tri = lax.broadcasted_iota(jnp.int32, (QB, QB), 0) >= lax.broadcasted_iota(jnp.int32, (QB, QB), 1)
    for qb in range(length // QB):
        r0 = qb * QB
        kend = r0 + QB
        q = q_ref[r0:kend, :]
        outs, lses = [], []
        for h in range(2):
            qm = jnp.where(low if h == 0 else ~low, q, jnp.zeros_like(q))
            sd = dot(qm, k_ref[r0:kend, :], NT)
            sd = jnp.where(tri, sd, -1e30)
            m = jnp.max(sd, axis=-1, keepdims=True)
            if qb:
                so = dot(qm, k_ref[:r0, :], NT)
                m = jnp.maximum(m, jnp.max(so, axis=-1, keepdims=True))
            pd = jnp.exp(sd - m)
            l = jnp.sum(pd, axis=-1, keepdims=True)
            o = dot(pd.astype(bf16), v_ref[r0:kend, :], NN)
            if qb:
                po = jnp.exp(so - m)
                l = l + jnp.sum(po, axis=-1, keepdims=True)
                o = o + dot(po.astype(bf16), v_ref[:r0, :], NN)
            outs.append(o / l)
            lses.append(m + jnp.log(l))
        o_ref[r0:kend, :] = jnp.where(low, outs[0], outs[1]).astype(bf16)
        lse_ref[0, r0:kend, :] = jnp.where(low, lses[0], lses[1])


def attn_fwd(qkv):
    length, w3 = qkv.shape
    pairs = w3 // 3 // 128
    blk = lambda off: pl.BlockSpec((length, 128), lambda i, off=off: (0, off + i))
    return pl.pallas_call(
        attn_fwd_kernel,
        grid=(pairs,),
        in_specs=[blk(0), blk(pairs), blk(2 * pairs)],
        out_specs=[pl.BlockSpec((length, 128), lambda i: (0, i)), pl.BlockSpec((1, length, 128), lambda i: (i, 0, 0))],
        out_shape=[jax.ShapeDtypeStruct((length, pairs * 128), bf16), jax.ShapeDtypeStruct((pairs, length, 128), f32)],
        cost_estimate=pl.CostEstimate(flops=20 * 10**9, transcendentals=10**7, bytes_accessed=16 * 2**20),
        name="attn_fwd",
    )(qkv, qkv, qkv)


def attn_bwd_kernel(q_ref, k_ref, v_ref, do_ref, o_ref, lse_ref, cos_ref, sin_ref, dq_ref, dk_ref, dv_ref, dk_acc, dv_acc):
    length = q_ref.shape[0]
    lane = lax.broadcasted_iota(jnp.int32, (1, 128), 1)
    low = lane < 64
    low32 = (lane % 64) < 32
    tri = lax.broadcasted_iota(jnp.int32, (QB, QB), 0) >= lax.broadcasted_iota(jnp.int32, (QB, QB), 1)
    for qb in range(length // QB):
        r0 = qb * QB
        kend = r0 + QB
        q = q_ref[r0:kend, :]
        do = do_ref[r0:kend, :]
        prod = do.astype(f32) * o_ref[r0:kend, :].astype(f32)
        lse2 = lse_ref[0, r0:kend, :]
        dq = jnp.zeros((QB, 128), f32)
        for h in range(2):
            sel = low if h == 0 else ~low
            qm = jnp.where(sel, q, jnp.zeros_like(q))
            dom = jnp.where(sel, do, jnp.zeros_like(do))
            delta = jnp.sum(jnp.where(sel, prod, 0.0), axis=-1, keepdims=True)
            lse = lse2[:, 64 * h:64 * h + 1]
            for kb in range(qb + 1):
                c0 = kb * QB
                k = k_ref[c0:c0 + QB, :]
                km = jnp.where(sel, k, jnp.zeros_like(k))
                s = dot(qm, k, NT)
                p = jnp.exp(s - lse)
                if kb == qb:
                    p = jnp.where(tri, p, 0.0)
                dp = dot(dom, v_ref[c0:c0 + QB, :], NT)
                ds = (p * (dp - delta)).astype(bf16)
                dvp = dot(p.astype(bf16), dom, TN)
                dkp = dot(ds, qm, TN)
                dq = dq + dot(ds, km, NN)
                if kb == qb and h == 0:
                    dv_acc[c0:c0 + QB, :] = dvp
                    dk_acc[c0:c0 + QB, :] = dkp
                else:
                    dv_acc[c0:c0 + QB, :] += dvp
                    dk_acc[c0:c0 + QB, :] += dkp
        dq_ref[r0:kend, :] = turn(dq * 0.125, cos_ref[r0:kend, :], sin_ref[r0:kend, :], low32).astype(bf16)
    dk_ref[...] = turn(dk_acc[...], cos_ref[...], sin_ref[...], low32).astype(bf16)
    dv_ref[...] = dv_acc[...].astype(bf16)


def attn_bwd(qkv, do, o, lse, cos, sin_back):
    length, w3 = qkv.shape
    pairs = w3 // 3 // 128
    blk = lambda off: pl.BlockSpec((length, 128), lambda i, off=off: (0, off + i))
    whole = pl.BlockSpec((length, 128), lambda i: (0, 0))
    return pl.pallas_call(
        attn_bwd_kernel,
        grid=(pairs,),
        in_specs=[blk(0), blk(pairs), blk(2 * pairs), blk(0), blk(0), pl.BlockSpec((1, length, 128), lambda i: (i, 0, 0)), whole, whole],
        out_specs=[blk(0)] * 3,
        out_shape=[jax.ShapeDtypeStruct((length, pairs * 128), bf16)] * 3,
        scratch_shapes=[pltpu.VMEM((length, 128), f32)] * 2,
        cost_estimate=pl.CostEstimate(flops=50 * 10**9, transcendentals=10**7, bytes_accessed=24 * 2**20),
        name="attn_bwd",
    )(qkv, qkv, qkv, do, o, lse, cos, sin_back)


def layer_norm(value, gain, shift):
    c = value - jnp.mean(value, axis=-1, keepdims=True)
    r = lax.rsqrt(jnp.mean(c * c, axis=-1, keepdims=True) + epsilon)
    return c * r * gain + shift


def tables(length):
    half = HEAD // 2
    places = jnp.arange(length, dtype=f32)[:, None]
    speeds = jnp.exp(jnp.arange(half, dtype=f32) * (-math.log(10000.0) / half))
    angles = places * speeds[None, :]
    cosine, sine = jnp.cos(angles), jnp.sin(angles)
    return jnp.concatenate([cosine] * 4, axis=1), jnp.concatenate([-sine, sine] * 2, axis=1)


def layer(dp, fsdp):
    outer, inner = all_bits(dp, fsdp)
    core, across, far = outer[0], outer[1:2], outer[2:]
    side, deep = inner[-1:], inner[:-1]
    early = far[::-1] + deep
    gather_a = early + side + across + [core]
    gather_b = early + across + side + [core]

    def on_device(tokens, w_qkv, w_out, w_up, w_down, gain_one, shift_one, gain_two, attention_norm_bias,
                  gain_three, shift_three, gain_four, shift_four, group_ids, group_weight, out_grad):
        seqs, length, width = tokens.shape
        rows = seqs * length
        packed = jnp.stack([gain_one, shift_one, gain_two, attention_norm_bias,
                            gain_three, shift_three, gain_four, shift_four])
        vectors = spread_vectors(packed, inner).astype(f32)
        full_qkv = jnp.concatenate([gather_rows(w_qkv[:, :w_qkv.shape[1] // 2], gather_a),
                                    gather_rows(w_qkv[:, w_qkv.shape[1] // 2:], gather_b)], axis=1)
        full_out = gather_rows(w_out, gather_a)
        full_up = gather_rows(w_up, gather_b)
        full_down = gather_rows(w_down, gather_a)
        cos, sin = tables(length)
        x = tokens.reshape(rows, width)
        normed_one, qkv = qkv_call(x, vectors[0:1], vectors[1:2], full_qkv, cos, sin)
        attended, lse = attn_fwd(qkv)
        inputs = x.astype(f32)
        branch_one = dot(attended, full_out, NN)
        after_one = inputs + layer_norm(branch_one, vectors[2], vectors[3])
        normed_two = layer_norm(after_one, vectors[4], vectors[5]).astype(bf16)
        hidden = dot(normed_two, full_up, NN)
        active, gelu_pull = jax.vjp(lambda h: jax.nn.gelu(h, approximate=True), hidden)
        active = active.astype(bf16)
        branch_two = dot(active, full_down, NN)
        activations = (after_one + layer_norm(branch_two, vectors[6], vectors[7])).astype(bf16)

        selected = (group_ids[:, None] == jnp.arange(GROUPS, dtype=jnp.int32)[None, :]).astype(f32)
        row_scale = jnp.sum(selected * group_weight[None, :], axis=1)
        incoming = (out_grad.astype(f32) * row_scale[:, None, None]).reshape(rows, width)
        pull = jax.vjp(layer_norm, branch_two, vectors[6], vectors[7])[1]
        grad_branch_two, grad_gain_four, grad_shift_four = pull(incoming)
        grad_two = grad_branch_two.astype(bf16)
        grad_active = dot(grad_two, full_down, NT)
        grad_hidden = gelu_pull(grad_active)[0].astype(bf16)
        grad_down = reduce_rows(dot(active, grad_two, TN).astype(bf16), gather_a[::-1])
        grad_up = reduce_rows(dot(normed_two, grad_hidden, TN).astype(bf16), gather_b[::-1])
        grad_normed_two = dot(grad_hidden, full_up, NT)
        pull = jax.vjp(layer_norm, after_one, vectors[4], vectors[5])[1]
        grad_after_part, grad_gain_three, grad_shift_three = pull(grad_normed_two)
        grad_after = incoming + grad_after_part
        pull = jax.vjp(layer_norm, branch_one, vectors[2], vectors[3])[1]
        grad_branch_one, grad_gain_two, grad_shift_two = pull(grad_after)
        grad_one = grad_branch_one.astype(bf16)
        grad_out = reduce_rows(dot(attended, grad_one, TN).astype(bf16), gather_a[::-1])
        grad_attended = dot(grad_one, full_out, NT).astype(bf16)
        grad_mixed = jnp.concatenate(attn_bwd(qkv, grad_attended, attended, lse, cos, -sin), axis=1)
        grad_wqkv = dot(normed_one, grad_mixed, TN).astype(bf16)
        mid = grad_wqkv.shape[1] // 2
        grad_qkv = jnp.concatenate([reduce_rows(grad_wqkv[:, :mid], gather_a[::-1]),
                                    reduce_rows(grad_wqkv[:, mid:], gather_b[::-1])], axis=1)
        grad_normed_one = dot(grad_mixed, full_qkv, NT)
        pull = jax.vjp(layer_norm, inputs, vectors[0], vectors[1])[1]
        grad_in_part, grad_gain_one, grad_shift_one = pull(grad_normed_one)
        input_grad = (grad_after + grad_in_part).reshape(seqs, length, width)
        sums = sum_vectors(jnp.stack([grad_gain_one, grad_shift_one, grad_gain_two, grad_shift_two,
                                      grad_gain_three, grad_shift_three, grad_gain_four, grad_shift_four]),
                           outer, inner)
        return (activations.reshape(seqs, length, width), input_grad, grad_qkv, grad_out, grad_up, grad_down,
                *[sums[k] for k in range(8)])

    return on_device


def solution(mesh):
    both = ("dp", "fsdp")
    rows3, rows2, part = P(both, None, None), P(both, None), P("fsdp")
    in_specs = (rows3, rows2, rows2, rows2, rows2) + (part,) * 8 + (P(both), P(), rows3)
    out_specs = (rows3, rows3, rows2, rows2, rows2, rows2) + (part,) * 8
    step = layer(mesh.shape["dp"], mesh.shape["fsdp"])
    return jax.shard_map(step, mesh=mesh, in_specs=in_specs, out_specs=out_specs, check_vma=False)
```
